32 devices in a mesh: row: 4 (over z), phi: 8 (over y, x, core).
Axes of the slice: x: 2, y: 2, z: 4, core: 2. Of those that a mesh axis runs over, the one named last changes fastest.
Arguments:
- fields: float32 [5, 64, 64, 4096], P(None, 'row', None, 'phi'), may hold values from -6 to 6
- offsets: int32 [64], P('row'), may hold values from 0 to 4095
- fraction: float32 [64], P('row'), may hold values from 0 to 1
- radial_diff: float32 [64], P('row'), may hold values from 0.05 to 0.15
- radial_drift: float32 [64], P('row'), may hold values from -0.05 to 0.05
- loop_diff: float32 [64], P('row'), may hold values from 0.05 to 0.15
- height_diff: float32 [64], replicated, may hold values from 0.05 to 0.15
Outputs:
- evolved: float32 [5, 64, 64, 4096], P(None, 'row', None, 'phi')
The draws below stay inside these ranges and needn't reach their ends.
All inputs are finite; a program needn't handle non-finite values.
Results may differ from the reference program's by a relative error of at most 0.00002.
Values sent between devices are 32-bit elements; how exact they have to be, the bound alone decides.
A program may use at most 128 MiB of HBM per device.

```python
import jax
import jax.numpy as jnp

FIELDS = 5
NZ = 64
NPHI = 4096
HYDRO = 2
NR = 64


def plant(array, own_key, low, high):
    place = [jax.random.randint(jax.random.fold_in(own_key, axis), (), 0, length) for axis, length in enumerate(array.shape)]
    longest = array.shape.index(max(array.shape))
    neighbour = place[:longest] + [(place[longest] + 1) % array.shape[longest]] + place[longest + 1:]
    return array.at[tuple(place)].set(low).at[tuple(neighbour)].set(high)


def level_of(own_key, shape, shards, smallest, largest):
    gain = 1.0
    for dim, parts in shards:
        draws = jax.random.uniform(jax.random.fold_in(jax.random.fold_in(own_key, 6), dim), (parts,), jnp.float32, smallest / len(shards), largest / len(shards))
        gain = gain * jnp.repeat(jnp.exp(draws), shape[dim] // parts).reshape((-1,) + (1,) * (len(shape) - 1 - dim))
    return gain


def normal_values(rng, shape, scale, limit, split=(), kind=jnp.bfloat16):
    values = jax.random.normal(rng, shape, jnp.float32) * scale
    if len(split) > 0:
        values = level_of(rng, shape, split, -0.22, 0.18) * values
    return jnp.clip(values, min=-limit, max=limit).astype(kind)


def setup_inputs(seed: int = 0) -> dict:
    streams_of = jax.random.split(jax.random.key(seed), 8)
    fields = normal_values(streams_of[0], (FIELDS, NR, NZ, NPHI), 1.0, 6.0, ((1, 4), (3, 8)), jnp.float32)
    offsets = plant(jax.random.randint(streams_of[1], (NR,), 0, NPHI), jax.random.fold_in(streams_of[1], 1), 0, NPHI - 1).astype(jnp.int32)
    fraction = jnp.clip(1.0 * jax.random.uniform(streams_of[2], (NR,), jnp.float32) ** level_of(streams_of[2], (NR,), ((0, 4),), -0.2, 0.2), 0.0, 1.0)
    radial_diff = jnp.clip(0.05 + 0.10000001 * jax.random.uniform(streams_of[3], (NR,), jnp.float32) ** level_of(streams_of[3], (NR,), ((0, 4),), -0.2, 0.2), 0.05, 0.15)
    radial_drift = jnp.clip(jax.random.uniform(streams_of[4], (NR,), jnp.float32, -0.05, 0.05) * level_of(streams_of[4], (NR,), ((0, 4),), -0.4, 0.0), -0.05, 0.05)
    loop_diff = jnp.clip(0.05 + 0.10000001 * jax.random.uniform(streams_of[5], (NR,), jnp.float32) ** level_of(streams_of[5], (NR,), ((0, 4),), -0.2, 0.2), 0.05, 0.15)
    height_diff = jnp.clip(jax.random.uniform(streams_of[6], (NZ,), jnp.float32, 0.05, 0.15), 0.05, 0.15)
    return dict(fields=fields, offsets=offsets, fraction=fraction, radial_diff=radial_diff, radial_drift=radial_drift, loop_diff=loop_diff, height_diff=height_diff)


def combine(state, upper, lower, east, west, above, below, radial_diff, radial_drift, loop_diff, height_diff):
    w_rad = radial_diff[None, :, None, None]
    v_rad = radial_drift[None, :, None, None]
    a_loop = loop_diff[None, :, None, None]
    c_height = height_diff[None, None, :, None]
    result = state + w_rad * (upper - 2.0 * state + lower) + v_rad * (upper - lower)
    result = result + a_loop * (east - 2.0 * state + west)
    return result + c_height * (above - 2.0 * state + below)


def reference(fields, offsets, fraction, radial_diff, radial_drift, loop_diff, height_diff):
    cells = jnp.arange(NPHI, dtype=jnp.int32)
    first_index = (cells[None, :] - offsets[:, None]) % NPHI
    second_index = (first_index - 1) % NPHI
    part_one = jnp.take_along_axis(fields, first_index[None, :, None, :], axis=3)
    part_two = jnp.take_along_axis(fields, second_index[None, :, None, :], axis=3)
    weight = fraction[None, :, None, None]
    state = (1.0 - weight) * part_one + weight * part_two
    for substep in range(HYDRO):
        radial_pad = jnp.pad(state, ((0, 0), (1, 1), (0, 0), (0, 0)))
        height_pad = jnp.pad(state, ((0, 0), (0, 0), (1, 1), (0, 0)))
        east = jnp.roll(state, -1, axis=3)
        west = jnp.roll(state, 1, axis=3)
        state = combine(state, radial_pad[:, 2:], radial_pad[:, :-2], east, west,
                        height_pad[:, :, 2:], height_pad[:, :, :-2],
                        radial_diff, radial_drift, loop_diff, height_diff)
    return state
```

```python
import functools

import jax
import jax.numpy as jnp
from jax import lax
from jax.experimental import pallas as pl
from jax.experimental.pallas import tpu as pltpu
from jax.sharding import PartitionSpec as P

LANES = 128
HALO = 2
MESH = pl.DeviceIdType.MESH


def kernel(
    n,
    rows,
    offs_ref,
    coef_ref,
    height_ref,
    fields_ref,
    out_ref,
    *scratch,
):
    fields, radii, nz, width = fields_ref.shape
    per = radii // n
    tiles = width // LANES
    loop_tiles = tiles * n
    (
        loops,
        stage,
        pack,
        edge_stage,
        state,
        edges,
        extra,
        mid,
        outb,
        coefs,
        in_send,
        in_recv,
        back_send,
        back_recv,
        edge_send,
        edge_recv,
        halo_send,
        halo_recv,
        coef_sem,
        own_sem,
        out_sem,
    ) = scratch
    me = lax.axis_index("phi")
    row = lax.axis_index("row")
    has_low = row > 0
    has_high = row < rows - 1
    lane = lax.broadcasted_iota(jnp.int32, (nz, LANES), 1)
    zrow = lax.broadcasted_iota(jnp.int32, (nz, LANES), 0)

    barrier = pltpu.get_barrier_semaphore()
    for d in range(1, n):
        pl.semaphore_signal(
            barrier, inc=1, device_id={"phi": lax.rem(me + d, n)}, device_id_type=MESH
        )

    @pl.when(has_low)
    def _():
        pl.semaphore_signal(barrier, inc=1, device_id={"row": row - 1}, device_id_type=MESH)

    @pl.when(has_high)
    def _():
        pl.semaphore_signal(barrier, inc=1, device_id={"row": row + 1}, device_id_type=MESH)

    inner = jnp.logical_and(has_low, has_high)

    @pl.when(inner)
    def _():
        pl.semaphore_wait(barrier, n + 1)

    @pl.when(jnp.logical_not(inner))
    def _():
        pl.semaphore_wait(barrier, n)

    def in_own(f):
        return pltpu.make_async_copy(
            fields_ref.at[f, pl.ds(me * per, per)], loops.at[f, me], own_sem.at[f]
        )

    def in_copy(f, d):
        to = lax.rem(me + d, n)
        return pltpu.make_async_remote_copy(
            src_ref=fields_ref.at[f, pl.ds(to * per, per)],
            dst_ref=loops.at[f, me],
            send_sem=in_send.at[f, d],
            recv_sem=in_recv.at[f, d],
            device_id={"phi": to},
            device_id_type=MESH,
        )

    def back_copies(f, d):
        to = lax.rem(me + d, n)
        main = pltpu.make_async_remote_copy(
            src_ref=stage.at[f, to],
            dst_ref=state.at[f, pl.ds(HALO + me * per, per)],
            send_sem=back_send.at[f, d],
            recv_sem=back_recv.at[f, d],
            device_id={"phi": to},
            device_id_type=MESH,
        )
        edge = pltpu.make_async_remote_copy(
            src_ref=edge_stage.at[f, to],
            dst_ref=edges.at[f, me + 1],
            send_sem=edge_send.at[f, d],
            recv_sem=edge_recv.at[f, d],
            device_id={"phi": to},
            device_id_type=MESH,
        )
        return main, edge

    def back_own(f):
        return (
            pltpu.make_async_copy(
                stage.at[f, me], state.at[f, pl.ds(HALO + me * per, per)], back_send.at[f, 0]
            ),
            pltpu.make_async_copy(edge_stage.at[f, me], edges.at[f, me + 1], edge_send.at[f, 0]),
        )

    def halo_copies(f, low):
        side = 0 if low else 1
        source = HALO if low else radii
        target = radii + HALO if low else 0
        to = row - 1 if low else row + 1
        return (
            pltpu.make_async_remote_copy(
                src_ref=state.at[f, pl.ds(source, HALO)],
                dst_ref=state.at[f, pl.ds(target, HALO)],
                send_sem=halo_send.at[f, side, 0],
                recv_sem=halo_recv.at[f, side, 0],
                device_id={"row": to},
                device_id_type=MESH,
            ),
            pltpu.make_async_remote_copy(
                src_ref=edges.at[f, 1 if low else n],
                dst_ref=edges.at[f, n + 1 if low else 0],
                send_sem=halo_send.at[f, side, 1],
                recv_sem=halo_recv.at[f, side, 1],
                device_id={"row": to},
                device_id_type=MESH,
            ),
        )

    def coef_copy(low):
        side = 0 if low else 1
        return pltpu.make_async_remote_copy(
            src_ref=coef_ref.at[pl.ds(0 if low else radii - HALO, HALO)],
            dst_ref=coefs.at[pl.ds(radii + HALO if low else 0, HALO)],
            send_sem=coef_sem.at[side],
            recv_sem=coef_sem.at[2 + side],
            device_id={"row": row - 1 if low else row + 1},
            device_id_type=MESH,
        )

    for f in range(fields):
        for d in range(1, n):
            in_copy(f, d).start()
        in_own(f).start()

    @pl.when(has_low)
    def _():
        coef_copy(True).start()

    @pl.when(has_high)
    def _():
        coef_copy(False).start()

    coefs[pl.ds(HALO, radii)] = coef_ref[...]

    @pl.when(jnp.logical_not(has_low))
    def _():
        state[:, 0:HALO] = jnp.zeros((fields, HALO, nz, width), jnp.float32)
        edges[:, 0] = jnp.zeros(edges.shape[:1] + edges.shape[2:], jnp.float32)
        coefs[0:HALO] = jnp.zeros((HALO,) + coefs.shape[1:], jnp.float32)

    @pl.when(jnp.logical_not(has_high))
    def _():
        state[:, radii + HALO :] = jnp.zeros((fields, HALO, nz, width), jnp.float32)
        edges[:, n + 1] = jnp.zeros(edges.shape[:1] + edges.shape[2:], jnp.float32)
        coefs[radii + HALO :] = jnp.zeros((HALO,) + coefs.shape[1:], jnp.float32)

    lane8 = lax.broadcasted_iota(jnp.int32, (8, LANES), 1)

    def shift_field(f, carry):
        in_own(f).wait()
        for d in range(1, n):
            in_copy(f, d).wait_recv()

        def shift_loop(ri, carry):
            offset = jnp.broadcast_to(offs_ref[me * per + ri, 0:1, :], (8, LANES))
            weight = jnp.broadcast_to(coef_ref[me * per + ri, 4:5, :], (8, LANES))
            keep = 1.0 - weight
            fine = offset & (LANES - 1)

            def shift_rows(group, carry):
                z0 = pl.multiple_of(group * 8, 8)
                cells = [
                    loops[f, t // tiles, ri, pl.ds(z0, 8), (t % tiles) * LANES : (t % tiles + 1) * LANES]
                    for t in range(loop_tiles)
                ]
                step = 1
                while step < LANES:
                    taken = (offset & step) != 0
                    cells = [jnp.where(taken, pltpu.roll(c, step, 1), c) for c in cells]
                    step *= 2
                inside = lane8 < fine
                cells = [
                    jnp.where(inside, cells[t - 1], cells[t]) for t in range(loop_tiles)
                ]
                step = 1
                while step < loop_tiles:
                    taken = (offset & (step * LANES)) != 0
                    cells = [
                        jnp.where(taken, cells[t - step], cells[t]) for t in range(loop_tiles)
                    ]
                    step *= 2
                turned = [pltpu.roll(c, 1, 1) for c in cells]
                moved = [
                    keep * cells[t] + weight * jnp.where(lane8 == 0, turned[t - 1], turned[t])
                    for t in range(loop_tiles)
                ]
                for t in range(loop_tiles):
                    at = (t % tiles) * LANES
                    stage[f, t // tiles, ri, pl.ds(z0, 8), at : at + LANES] = moved[t]
                for q in range(n):
                    right = moved[(tiles * q + tiles) % loop_tiles]
                    both = jnp.where(lane8 < LANES // 2, right, moved[tiles * q - 1])
                    pack[ri, q, pl.ds(z0, 8), :] = both
                return carry

            return lax.fori_loop(0, nz // 8, shift_rows, carry)

        lax.fori_loop(0, per, shift_loop, 0)

        def pack_edges(q, carry):
            tile = pltpu.roll(pack[0, q], 2, 1)
            for ri in range(1, per):
                tile = jnp.where(lane < 4 * ri, tile, pltpu.roll(pack[ri, q], 2 + 4 * ri, 1))
            square = jnp.concatenate([tile] * (LANES // nz), axis=0).T
            edge_stage[f, q] = square[0 : 4 * per]
            return carry

        lax.fori_loop(0, n, pack_edges, 0)
        for copy in back_own(f):
            copy.start()
        for d in range(1, n):
            for copy in back_copies(f, d):
                copy.start()
        return carry

    lax.fori_loop(0, fields, shift_field, 0)

    @pl.when(has_low)
    def _():
        coef_copy(False).wait_recv()

    @pl.when(has_high)
    def _():
        coef_copy(True).wait_recv()

    def blend(cur, prev_tile, next_tile, up, low, where_r, height, height2):
        k_up = coefs[where_r, 0:1, :]
        k_low = coefs[where_r, 1:2, :]
        k_loop = coefs[where_r, 2:3, :]
        k_mid = coefs[where_r, 3:4, :]
        west = jnp.where(lane == 0, pltpu.roll(prev_tile, 1, 1), pltpu.roll(cur, 1, 1))
        east = jnp.where(
            lane == LANES - 1,
            pltpu.roll(next_tile, LANES - 1, 1),
            pltpu.roll(cur, LANES - 1, 1),
        )
        below = jnp.where(zrow == 0, 0.0, pltpu.roll(cur, 1, 0))
        above = jnp.where(zrow == nz - 1, 0.0, pltpu.roll(cur, nz - 1, 0))
        total = (k_mid - height2) * cur + k_up * up + k_low * low
        return total + k_loop * (east + west) + height * (above + below)

    def out_copy(f):
        return pltpu.make_async_copy(outb.at[f % 2], out_ref.at[f], out_sem.at[f % 2])

    for f in range(fields):
        for copy in back_own(f):
            copy.wait()
        for d in range(1, n):
            for copy in back_copies(f, d):
                copy.wait_recv()

        @pl.when(has_low)
        def _(f=f):
            for copy in halo_copies(f, True):
                copy.start()

        @pl.when(has_high)
        def _(f=f):
            for copy in halo_copies(f, False):
                copy.start()

        @pl.when(has_low)
        def _(f=f):
            for copy in halo_copies(f, False):
                copy.wait_recv()

        @pl.when(has_high)
        def _(f=f):
            for copy in halo_copies(f, True):
                copy.wait_recv()

        lines = edges[f].reshape((n + 2) * 4 * per, LANES)
        square = jnp.concatenate([lines, lines[0 : LANES - lines.shape[0]]], axis=0).T[0:nz]

        def spread(i, carry):
            extra[i] = pltpu.roll(square, LANES - 2 - 4 * i, 1)
            return carry

        lax.fori_loop(0, radii + 2 * HALO, spread, 0)

        def first(i, carry, f=f):
            height = height_ref[...]
            height2 = height + height

            def tile(r, t):
                if t == tiles:
                    return extra[r]
                return state[f, r, :, pl.ds(t * LANES, LANES)]

            for t in range(tiles + 1):
                mid[i - 1, :, pl.ds(t * LANES, LANES)] = blend(
                    tile(i, t),
                    tile(i, (t + tiles) % (tiles + 1)),
                    tile(i, (t + 1) % (tiles + 1)),
                    tile(i + 1, t),
                    tile(i - 1, t),
                    i,
                    height,
                    height2,
                )
            return carry

        lax.fori_loop(1, radii + 2 * HALO - 1, first, 0)

        @pl.when(jnp.logical_not(has_low))
        def _():
            mid[0] = jnp.zeros(mid.shape[1:], jnp.float32)

        @pl.when(jnp.logical_not(has_high))
        def _():
            mid[radii + 1] = jnp.zeros(mid.shape[1:], jnp.float32)

        if f >= 2:
            out_copy(f - 2).wait()

        def second(i, carry, f=f):
            height = height_ref[...]
            height2 = height + height

            def tile(r, t):
                return mid[r, :, pl.ds(t * LANES, LANES)]

            for t in range(tiles):
                outb[f % 2, i - 1, :, pl.ds(t * LANES, LANES)] = blend(
                    tile(i, t),
                    tile(i, (t + tiles) % (tiles + 1)),
                    tile(i, (t + 1) % (tiles + 1)),
                    tile(i + 1, t),
                    tile(i - 1, t),
                    i + 1,
                    height,
                    height2,
                )
            return carry

        lax.fori_loop(1, radii + 1, second, 0)
        out_copy(f).start()

    for f in range(max(fields - 2, 0), fields):
        out_copy(f).wait()
    for f in range(fields):
        for d in range(1, n):
            in_copy(f, d).wait_send()
            for copy in back_copies(f, d):
                copy.wait_send()

        @pl.when(has_low)
        def _(f=f):
            for copy in halo_copies(f, True):
                copy.wait_send()

        @pl.when(has_high)
        def _(f=f):
            for copy in halo_copies(f, False):
                copy.wait_send()

    @pl.when(has_low)
    def _():
        coef_copy(True).wait_send()

    @pl.when(has_high)
    def _():
        coef_copy(False).wait_send()


def local(n, rows, fields, offsets, fraction, radial_diff, radial_drift, loop_diff, height_diff):
    count, radii, nz, width = fields.shape
    per = radii // n
    full = radii + 2 * HALO
    wide = width + LANES
    table = jnp.stack(
        [
            radial_diff + radial_drift,
            radial_diff - radial_drift,
            loop_diff,
            1.0 - 2.0 * (radial_diff + loop_diff),
            fraction,
        ],
        axis=1,
    )
    table = jnp.pad(table, ((0, 0), (0, 3)))
    table = jnp.broadcast_to(table[:, :, None], (radii, 8, LANES))
    shifts = jnp.broadcast_to(offsets[:, None, None], (radii, 8, LANES))
    heights = jnp.broadcast_to(height_diff[:, None], (nz, LANES))
    f32 = jnp.float32
    dma = pltpu.SemaphoreType.DMA
    scratch = [
        pltpu.VMEM((count, n, per, nz, width), f32),
        pltpu.VMEM((count, n, per, nz, width), f32),
        pltpu.VMEM((per, n, nz, LANES), f32),
        pltpu.VMEM((count, n, 4 * per, LANES), f32),
        pltpu.VMEM((count, full, nz, width), f32),
        pltpu.VMEM((count, n + 2, 4 * per, LANES), f32),
        pltpu.VMEM((full, nz, LANES), f32),
        pltpu.VMEM((full - 2, nz, wide), f32),
        pltpu.VMEM((2, radii, nz, width), f32),
        pltpu.VMEM((full, 8, LANES), f32),
        dma((count, n)),
        dma((count, n)),
        dma((count, n)),
        dma((count, n)),
        dma((count, n)),
        dma((count, n)),
        dma((count, 2, 2)),
        dma((count, 2, 2)),
        dma((4,)),
        dma((count,)),
        dma((2,)),
    ]
    vmem = pl.BlockSpec(memory_space=pltpu.VMEM)
    hbm = pl.BlockSpec(memory_space=pl.ANY)
    return pl.pallas_call(
        functools.partial(kernel, n, rows),
        out_shape=jax.ShapeDtypeStruct(fields.shape, f32),
        in_specs=[vmem, vmem, vmem, hbm],
        out_specs=hbm,
        scratch_shapes=scratch,
        compiler_params=pltpu.CompilerParams(
            collective_id=0, has_side_effects=True, vmem_limit_bytes=60 * 1024 * 1024
        ),
    )(shifts, table, heights, fields)


def solution(mesh):
    placed = (P(None, "row", None, "phi"), P("row"), P("row"), P("row"), P("row"), P("row"), P())
    body = functools.partial(local, mesh.shape["phi"], mesh.shape["row"])
    return jax.shard_map(
        body, mesh=mesh, in_specs=placed, out_specs=P(None, "row", None, "phi"), check_vma=False
    )
```

```python
import functools

import jax
import jax.numpy as jnp
from jax import lax
from jax.experimental import pallas as pl
from jax.experimental.pallas import tpu as pltpu
from jax.sharding import PartitionSpec as P

LANES = 128
HALO = 2
MESH = pl.DeviceIdType.MESH


def kernel(
    n,
    rows,
    offs_in,
    frac_in,
    diff_in,
    drift_in,
    loop_in,
    rise_in,
    fields_ref,
    out_ref,
    *scratch,
):
    fields, radii, nz, width = fields_ref.shape
    per = radii // n
    tiles = width // LANES
    loop_tiles = tiles * n
    (
        loops,
        stage,
        pack,
        edge_stage,
        state,
        edges,
        extra,
        mid,
        coefs,
        height_ref,
        offs_ref,
        frac_ref,
        diff_ref,
        drift_ref,
        loop_ref,
        rise_ref,
        small_sem,
        in_send,
        in_recv,
        back_send,
        back_recv,
        edge_send,
        edge_recv,
        halo_send,
        halo_recv,
        coef_sem,
        own_sem,
    ) = scratch
    smalls = [
        pltpu.make_async_copy(source, target, small_sem.at[i])
        for i, (source, target) in enumerate(
            (
                (offs_in, offs_ref),
                (frac_in, frac_ref),
                (diff_in, diff_ref),
                (drift_in, drift_ref),
                (loop_in, loop_ref),
                (rise_in, rise_ref),
            )
        )
    ]
    for copy in smalls:
        copy.start()
    me = lax.axis_index("phi")
    row = lax.axis_index("row")
    has_low = row > 0
    has_high = row < rows - 1
    lane = lax.broadcasted_iota(jnp.int32, (nz, LANES), 1)
    zrow = lax.broadcasted_iota(jnp.int32, (nz, LANES), 0)

    barrier = pltpu.get_barrier_semaphore()
    for d in range(1, n):
        pl.semaphore_signal(
            barrier, inc=1, device_id={"phi": lax.rem(me + d, n)}, device_id_type=MESH
        )

    @pl.when(has_low)
    def _():
        pl.semaphore_signal(barrier, inc=1, device_id={"row": row - 1}, device_id_type=MESH)

    @pl.when(has_high)
    def _():
        pl.semaphore_signal(barrier, inc=1, device_id={"row": row + 1}, device_id_type=MESH)

    inner = jnp.logical_and(has_low, has_high)

    @pl.when(inner)
    def _():
        pl.semaphore_wait(barrier, n + 1)

    @pl.when(jnp.logical_not(inner))
    def _():
        pl.semaphore_wait(barrier, n)

    def in_own(f):
        return pltpu.make_async_copy(
            fields_ref.at[f, pl.ds(me * per, per)], loops.at[f, me], own_sem.at[f]
        )

    def in_copy(f, d):
        to = lax.rem(me + d, n)
        return pltpu.make_async_remote_copy(
            src_ref=fields_ref.at[f, pl.ds(to * per, per)],
            dst_ref=loops.at[f, me],
            send_sem=in_send.at[f, d],
            recv_sem=in_recv.at[f, d],
            device_id={"phi": to},
            device_id_type=MESH,
        )

    def back_copies(f, d):
        to = lax.rem(me + d, n)
        main = pltpu.make_async_remote_copy(
            src_ref=stage.at[f, to],
            dst_ref=state.at[f, pl.ds(HALO + me * per, per)],
            send_sem=back_send.at[f, d],
            recv_sem=back_recv.at[f, d],
            device_id={"phi": to},
            device_id_type=MESH,
        )
        edge = pltpu.make_async_remote_copy(
            src_ref=edge_stage.at[f, to],
            dst_ref=edges.at[f, me + 1],
            send_sem=edge_send.at[f, d],
            recv_sem=edge_recv.at[f, d],
            device_id={"phi": to},
            device_id_type=MESH,
        )
        return main, edge

    def back_own(f):
        return (
            pltpu.make_async_copy(
                stage.at[f, me], state.at[f, pl.ds(HALO + me * per, per)], back_send.at[f, 0]
            ),
            pltpu.make_async_copy(edge_stage.at[f, me], edges.at[f, me + 1], edge_send.at[f, 0]),
        )

    def halo_copies(f, low):
        side = 0 if low else 1
        source = HALO if low else radii
        target = radii + HALO if low else 0
        to = row - 1 if low else row + 1
        return (
            pltpu.make_async_remote_copy(
                src_ref=state.at[f, pl.ds(source, HALO)],
                dst_ref=state.at[f, pl.ds(target, HALO)],
                send_sem=halo_send.at[f, side, 0],
                recv_sem=halo_recv.at[f, side, 0],
                device_id={"row": to},
                device_id_type=MESH,
            ),
            pltpu.make_async_remote_copy(
                src_ref=edges.at[f, 1 if low else n],
                dst_ref=edges.at[f, n + 1 if low else 0],
                send_sem=halo_send.at[f, side, 1],
                recv_sem=halo_recv.at[f, side, 1],
                device_id={"row": to},
                device_id_type=MESH,
            ),
        )

    def coef_copy(low):
        side = 0 if low else 1
        return pltpu.make_async_remote_copy(
            src_ref=coefs.at[pl.ds(HALO if low else radii, HALO)],
            dst_ref=coefs.at[pl.ds(radii + HALO if low else 0, HALO)],
            send_sem=coef_sem.at[side],
            recv_sem=coef_sem.at[2 + side],
            device_id={"row": row - 1 if low else row + 1},
            device_id_type=MESH,
        )

    for f in range(fields):
        for d in range(1, n):
            in_copy(f, d).start()
        in_own(f).start()

    for copy in smalls:
        copy.wait()

    def fill_coefs(i, carry):
        diff = jnp.full((1, LANES), diff_ref[i], jnp.float32)
        drift = jnp.full((1, LANES), drift_ref[i], jnp.float32)
        loop = jnp.full((1, LANES), loop_ref[i], jnp.float32)
        coefs[HALO + i, 0:1, :] = diff + drift
        coefs[HALO + i, 1:2, :] = diff - drift
        coefs[HALO + i, 2:3, :] = loop
        coefs[HALO + i, 3:4, :] = 1.0 - 2.0 * (diff + loop)
        coefs[HALO + i, 4:5, :] = jnp.full((1, LANES), frac_ref[i], jnp.float32)
        coefs[HALO + i, 5:8, :] = jnp.zeros((3, LANES), jnp.float32)
        return carry

    lax.fori_loop(0, radii, fill_coefs, 0)

    def fill_height(z, carry):
        height_ref[pl.ds(z, 1), :] = jnp.full((1, LANES), rise_ref[z], jnp.float32)
        return carry

    lax.fori_loop(0, nz, fill_height, 0)

    @pl.when(has_low)
    def _():
        coef_copy(True).start()

    @pl.when(has_high)
    def _():
        coef_copy(False).start()


    @pl.when(jnp.logical_not(has_low))
    def _():
        state[:, 0:HALO] = jnp.zeros((fields, HALO, nz, width), jnp.float32)
        edges[:, 0] = jnp.zeros(edges.shape[:1] + edges.shape[2:], jnp.float32)
        coefs[0:HALO] = jnp.zeros((HALO,) + coefs.shape[1:], jnp.float32)

    @pl.when(jnp.logical_not(has_high))
    def _():
        state[:, radii + HALO :] = jnp.zeros((fields, HALO, nz, width), jnp.float32)
        edges[:, n + 1] = jnp.zeros(edges.shape[:1] + edges.shape[2:], jnp.float32)
        coefs[radii + HALO :] = jnp.zeros((HALO,) + coefs.shape[1:], jnp.float32)

    lane8 = lax.broadcasted_iota(jnp.int32, (8, LANES), 1)

    def shift_field(f, carry):
        in_own(f).wait()
        for d in range(1, n):
            in_copy(f, d).wait_recv()

        def shift_loop(ri, carry):
            offset = jnp.full((8, LANES), offs_ref[me * per + ri], jnp.int32)
            weight = jnp.broadcast_to(coefs[HALO + me * per + ri, 4:5, :], (8, LANES))
            keep = 1.0 - weight
            fine = offset & (LANES - 1)

            def shift_rows(group, carry):
                z0 = pl.multiple_of(group * 8, 8)
                cells = [
                    loops[f, t // tiles, ri, pl.ds(z0, 8), (t % tiles) * LANES : (t % tiles + 1) * LANES]
                    for t in range(loop_tiles)
                ]
                step = 1
                while step < LANES:
                    taken = (offset & step) != 0
                    cells = [jnp.where(taken, pltpu.roll(c, step, 1), c) for c in cells]
                    step *= 2
                inside = lane8 < fine
                cells = [
                    jnp.where(inside, cells[t - 1], cells[t]) for t in range(loop_tiles)
                ]
                step = 1
                while step < loop_tiles:
                    taken = (offset & (step * LANES)) != 0
                    cells = [
                        jnp.where(taken, cells[t - step], cells[t]) for t in range(loop_tiles)
                    ]
                    step *= 2
                turned = [pltpu.roll(c, 1, 1) for c in cells]
                moved = [
                    keep * cells[t] + weight * jnp.where(lane8 == 0, turned[t - 1], turned[t])
                    for t in range(loop_tiles)
                ]
                for t in range(loop_tiles):
                    at = (t % tiles) * LANES
                    stage[f, t // tiles, ri, pl.ds(z0, 8), at : at + LANES] = moved[t]
                for q in range(n):
                    right = moved[(tiles * q + tiles) % loop_tiles]
                    both = jnp.where(lane8 < LANES // 2, right, moved[tiles * q - 1])
                    pack[ri, q, pl.ds(z0, 8), :] = both
                return carry

            return lax.fori_loop(0, nz // 8, shift_rows, carry)

        lax.fori_loop(0, per, shift_loop, 0)

        def pack_edges(q, carry):
            tile = pltpu.roll(pack[0, q], 2, 1)
            for ri in range(1, per):
                tile = jnp.where(lane < 4 * ri, tile, pltpu.roll(pack[ri, q], 2 + 4 * ri, 1))
            square = jnp.concatenate([tile] * (LANES // nz), axis=0).T
            edge_stage[f, q] = square[0 : 4 * per]
            return carry

        lax.fori_loop(0, n, pack_edges, 0)
        for copy in back_own(f):
            copy.start()
        for d in range(1, n):
            for copy in back_copies(f, d):
                copy.start()
        return carry

    lax.fori_loop(0, fields, shift_field, 0)

    @pl.when(has_low)
    def _():
        coef_copy(False).wait_recv()

    @pl.when(has_high)
    def _():
        coef_copy(True).wait_recv()

    def blend(cur, prev_tile, next_tile, up, low, where_r, height, height2):
        k_up = coefs[where_r, 0:1, :]
        k_low = coefs[where_r, 1:2, :]
        k_loop = coefs[where_r, 2:3, :]
        k_mid = coefs[where_r, 3:4, :]
        west = jnp.where(lane == 0, pltpu.roll(prev_tile, 1, 1), pltpu.roll(cur, 1, 1))
        east = jnp.where(
            lane == LANES - 1,
            pltpu.roll(next_tile, LANES - 1, 1),
            pltpu.roll(cur, LANES - 1, 1),
        )
        below = jnp.where(zrow == 0, 0.0, pltpu.roll(cur, 1, 0))
        above = jnp.where(zrow == nz - 1, 0.0, pltpu.roll(cur, nz - 1, 0))
        total = (k_mid - height2) * cur + k_up * up + k_low * low
        return total + k_loop * (east + west) + height * (above + below)

    for f in range(fields):
        for copy in back_own(f):
            copy.wait()
        for d in range(1, n):
            for copy in back_copies(f, d):
                copy.wait_recv()

        @pl.when(has_low)
        def _(f=f):
            for copy in halo_copies(f, True):
                copy.start()

        @pl.when(has_high)
        def _(f=f):
            for copy in halo_copies(f, False):
                copy.start()

        @pl.when(has_low)
        def _(f=f):
            for copy in halo_copies(f, False):
                copy.wait_recv()

        @pl.when(has_high)
        def _(f=f):
            for copy in halo_copies(f, True):
                copy.wait_recv()

        lines = edges[f].reshape((n + 2) * 4 * per, LANES)
        square = jnp.concatenate([lines, lines[0 : LANES - lines.shape[0]]], axis=0).T[0:nz]

        def spread(i, carry):
            extra[i] = pltpu.roll(square, LANES - 2 - 4 * i, 1)
            return carry

        lax.fori_loop(0, radii + 2 * HALO, spread, 0)

        def first(i, carry, f=f):
            height = height_ref[...]
            height2 = height + height

            def tile(r, t):
                if t == tiles:
                    return extra[r]
                return state[f, r, :, pl.ds(t * LANES, LANES)]

            for t in range(tiles + 1):
                mid[i - 1, :, pl.ds(t * LANES, LANES)] = blend(
                    tile(i, t),
                    tile(i, (t + tiles) % (tiles + 1)),
                    tile(i, (t + 1) % (tiles + 1)),
                    tile(i + 1, t),
                    tile(i - 1, t),
                    i,
                    height,
                    height2,
                )
            return carry

        lax.fori_loop(1, radii + 2 * HALO - 1, first, 0)

        @pl.when(jnp.logical_not(has_low))
        def _():
            mid[0] = jnp.zeros(mid.shape[1:], jnp.float32)

        @pl.when(jnp.logical_not(has_high))
        def _():
            mid[radii + 1] = jnp.zeros(mid.shape[1:], jnp.float32)

        def second(i, carry, f=f):
            height = height_ref[...]
            height2 = height + height

            def tile(r, t):
                return mid[r, :, pl.ds(t * LANES, LANES)]

            for t in range(tiles):
                out_ref[f, i - 1, :, pl.ds(t * LANES, LANES)] = blend(
                    tile(i, t),
                    tile(i, (t + tiles) % (tiles + 1)),
                    tile(i, (t + 1) % (tiles + 1)),
                    tile(i + 1, t),
                    tile(i - 1, t),
                    i + 1,
                    height,
                    height2,
                )
            return carry

        lax.fori_loop(1, radii + 1, second, 0)

    for f in range(fields):
        for d in range(1, n):
            in_copy(f, d).wait_send()
            for copy in back_copies(f, d):
                copy.wait_send()

        @pl.when(has_low)
        def _(f=f):
            for copy in halo_copies(f, True):
                copy.wait_send()

        @pl.when(has_high)
        def _(f=f):
            for copy in halo_copies(f, False):
                copy.wait_send()

    @pl.when(has_low)
    def _():
        coef_copy(True).wait_send()

    @pl.when(has_high)
    def _():
        coef_copy(False).wait_send()


def local(n, rows, fields, offsets, fraction, radial_diff, radial_drift, loop_diff, height_diff):
    count, radii, nz, width = fields.shape
    per = radii // n
    full = radii + 2 * HALO
    wide = width + LANES
    f32 = jnp.float32
    dma = pltpu.SemaphoreType.DMA
    scratch = [
        pltpu.VMEM((count, n, per, nz, width), f32),
        pltpu.VMEM((count, n, per, nz, width), f32),
        pltpu.VMEM((per, n, nz, LANES), f32),
        pltpu.VMEM((count, n, 4 * per, LANES), f32),
        pltpu.VMEM((count, full, nz, width), f32),
        pltpu.VMEM((count, n + 2, 4 * per, LANES), f32),
        pltpu.VMEM((full, nz, LANES), f32),
        pltpu.VMEM((full - 2, nz, wide), f32),
        pltpu.VMEM((full, 8, LANES), f32),
        pltpu.VMEM((nz, LANES), f32),
        pltpu.SMEM((radii,), jnp.int32),
        pltpu.SMEM((radii,), f32),
        pltpu.SMEM((radii,), f32),
        pltpu.SMEM((radii,), f32),
        pltpu.SMEM((radii,), f32),
        pltpu.SMEM((nz,), f32),
        dma((6,)),
        dma((count, n)),
        dma((count, n)),
        dma((count, n)),
        dma((count, n)),
        dma((count, n)),
        dma((count, n)),
        dma((count, 2, 2)),
        dma((count, 2, 2)),
        dma((4,)),
        dma((count,)),
    ]
    hbm = pl.BlockSpec(memory_space=pltpu.HBM)
    return pl.pallas_call(
        functools.partial(kernel, n, rows),
        out_shape=pltpu.VMEM(fields.shape, f32),
        in_specs=[hbm] * 7,
        out_specs=pl.BlockSpec(memory_space=pltpu.VMEM),
        scratch_shapes=scratch,
        compiler_params=pltpu.CompilerParams(
            collective_id=0, has_side_effects=True, vmem_limit_bytes=42 * 1024 * 1024
        ),
    )(offsets, fraction, radial_diff, radial_drift, loop_diff, height_diff, fields)


def solution(mesh):
    placed = (P(None, "row", None, "phi"), P("row"), P("row"), P("row"), P("row"), P("row"), P())
    body = functools.partial(local, mesh.shape["phi"], mesh.shape["row"])
    return jax.shard_map(
        body, mesh=mesh, in_specs=placed, out_specs=P(None, "row", None, "phi"), check_vma=False
    )
```

```python
import functools

import jax
import jax.numpy as jnp
from jax import lax
from jax.experimental import pallas as pl
from jax.experimental.pallas import tpu as pltpu
from jax.sharding import PartitionSpec as P

LANES = 128
HALO = 2
MESH = pl.DeviceIdType.MESH


def kernel(
    n,
    rows,
    offs_in,
    frac_in,
    diff_in,
    drift_in,
    loop_in,
    rise_in,
    fields_ref,
    out_ref,
    *scratch,
):
    fields, radii, nz, width = fields_ref.shape
    per = radii // n
    half = n // 2
    tiles = width // LANES
    loop_tiles = tiles * n
    (
        loops,
        stage,
        pack,
        edge_stage,
        state,
        edges,
        extra,
        mid,
        coefs,
        height_ref,
        offs_ref,
        frac_ref,
        diff_ref,
        drift_ref,
        loop_ref,
        rise_ref,
        small_sem,
        in_send,
        in_recv,
        back_send,
        back_recv,
        edge_send,
        edge_recv,
        halo_send,
        halo_recv,
        coef_sem,
        own_sem,
    ) = scratch
    smalls = [
        pltpu.make_async_copy(source, target, small_sem.at[i])
        for i, (source, target) in enumerate(
            (
                (offs_in, offs_ref),
                (frac_in, frac_ref),
                (diff_in, diff_ref),
                (drift_in, drift_ref),
                (loop_in, loop_ref),
                (rise_in, rise_ref),
            )
        )
    ]
    for copy in smalls:
        copy.start()
    me = lax.axis_index("phi")
    row = lax.axis_index("row")
    has_low = row > 0
    has_high = row < rows - 1
    lane = lax.broadcasted_iota(jnp.int32, (nz, LANES), 1)
    zrow = lax.broadcasted_iota(jnp.int32, (nz, LANES), 0)

    barrier = pltpu.get_barrier_semaphore()
    for d in range(1, n):
        pl.semaphore_signal(
            barrier, inc=1, device_id={"phi": lax.rem(me + d, n)}, device_id_type=MESH
        )

    @pl.when(has_low)
    def _():
        pl.semaphore_signal(barrier, inc=1, device_id={"row": row - 1}, device_id_type=MESH)

    @pl.when(has_high)
    def _():
        pl.semaphore_signal(barrier, inc=1, device_id={"row": row + 1}, device_id_type=MESH)

    inner = jnp.logical_and(has_low, has_high)

    @pl.when(inner)
    def _():
        pl.semaphore_wait(barrier, n + 1)

    @pl.when(jnp.logical_not(inner))
    def _():
        pl.semaphore_wait(barrier, n)

    def radius(owner, ri):
        if ri == 1:
            return owner + half
        return jnp.where(owner < half, owner, owner + radii - n)

    def in_own(f, ri):
        return pltpu.make_async_copy(
            fields_ref.at[f, radius(me, ri)], loops.at[f, me, ri], own_sem.at[f, ri]
        )

    def in_copy(f, ri, d):
        to = lax.rem(me + d, n)
        return pltpu.make_async_remote_copy(
            src_ref=fields_ref.at[f, radius(to, ri)],
            dst_ref=loops.at[f, me, ri],
            send_sem=in_send.at[f, ri, d],
            recv_sem=in_recv.at[f, ri, d],
            device_id={"phi": to},
            device_id_type=MESH,
        )

    def back_copy(f, ri, d):
        to = lax.rem(me + d, n)
        return pltpu.make_async_remote_copy(
            src_ref=stage.at[f, to, ri],
            dst_ref=state.at[f, HALO + radius(me, ri)],
            send_sem=back_send.at[f, ri, d],
            recv_sem=back_recv.at[f, ri, d],
            device_id={"phi": to},
            device_id_type=MESH,
        )

    def edge_copy(f, d):
        to = lax.rem(me + d, n)
        return pltpu.make_async_remote_copy(
            src_ref=edge_stage.at[f, to],
            dst_ref=edges.at[f, me + HALO],
            send_sem=edge_send.at[f, d],
            recv_sem=edge_recv.at[f, d],
            device_id={"phi": to},
            device_id_type=MESH,
        )

    def back_own(f, ri):
        return pltpu.make_async_copy(
            stage.at[f, me, ri], state.at[f, HALO + radius(me, ri)], back_send.at[f, ri, 0]
        )

    def edge_own(f):
        return pltpu.make_async_copy(
            edge_stage.at[f, me], edges.at[f, me + HALO], edge_send.at[f, 0]
        )

    def halo_copies(f, low):
        side = 0 if low else 1
        source = HALO if low else radii
        target = radii + HALO if low else 0
        to = row - 1 if low else row + 1
        return (
            pltpu.make_async_remote_copy(
                src_ref=state.at[f, pl.ds(source, HALO)],
                dst_ref=state.at[f, pl.ds(target, HALO)],
                send_sem=halo_send.at[f, side, 0],
                recv_sem=halo_recv.at[f, side, 0],
                device_id={"row": to},
                device_id_type=MESH,
            ),
            pltpu.make_async_remote_copy(
                src_ref=edges.at[f, pl.ds(HALO if low else n, HALO)],
                dst_ref=edges.at[f, pl.ds(n + HALO if low else 0, HALO)],
                send_sem=halo_send.at[f, side, 1],
                recv_sem=halo_recv.at[f, side, 1],
                device_id={"row": to},
                device_id_type=MESH,
            ),
        )

    def coef_copy(low):
        side = 0 if low else 1
        return pltpu.make_async_remote_copy(
            src_ref=coefs.at[pl.ds(HALO if low else radii, HALO)],
            dst_ref=coefs.at[pl.ds(radii + HALO if low else 0, HALO)],
            send_sem=coef_sem.at[side],
            recv_sem=coef_sem.at[2 + side],
            device_id={"row": row - 1 if low else row + 1},
            device_id_type=MESH,
        )

    for f in range(fields):
        for ri in range(per):
            for d in range(1, n):
                in_copy(f, ri, d).start()
            in_own(f, ri).start()

    for copy in smalls:
        copy.wait()

    def fill_coefs(i, carry):
        diff = jnp.full((1, LANES), diff_ref[i], jnp.float32)
        drift = jnp.full((1, LANES), drift_ref[i], jnp.float32)
        loop = jnp.full((1, LANES), loop_ref[i], jnp.float32)
        coefs[HALO + i, 0:1, :] = diff + drift
        coefs[HALO + i, 1:2, :] = diff - drift
        coefs[HALO + i, 2:3, :] = loop
        coefs[HALO + i, 3:4, :] = 1.0 - 2.0 * (diff + loop)
        coefs[HALO + i, 4:5, :] = jnp.full((1, LANES), frac_ref[i], jnp.float32)
        coefs[HALO + i, 5:8, :] = jnp.zeros((3, LANES), jnp.float32)
        return carry

    lax.fori_loop(0, radii, fill_coefs, 0)

    def fill_height(z, carry):
        height_ref[pl.ds(z, 1), :] = jnp.full((1, LANES), rise_ref[z], jnp.float32)
        return carry

    lax.fori_loop(0, nz, fill_height, 0)

    @pl.when(has_low)
    def _():
        coef_copy(True).start()

    @pl.when(has_high)
    def _():
        coef_copy(False).start()


    @pl.when(jnp.logical_not(has_low))
    def _():
        state[:, 0:HALO] = jnp.zeros((fields, HALO, nz, width), jnp.float32)
        edges[:, 0:HALO] = jnp.zeros((fields, HALO) + edges.shape[2:], jnp.float32)
        coefs[0:HALO] = jnp.zeros((HALO,) + coefs.shape[1:], jnp.float32)

    @pl.when(jnp.logical_not(has_high))
    def _():
        state[:, radii + HALO :] = jnp.zeros((fields, HALO, nz, width), jnp.float32)
        edges[:, n + HALO :] = jnp.zeros((fields, HALO) + edges.shape[2:], jnp.float32)
        coefs[radii + HALO :] = jnp.zeros((HALO,) + coefs.shape[1:], jnp.float32)

    lane8 = lax.broadcasted_iota(jnp.int32, (8, LANES), 1)

    def shift_field(f, carry):
        for ri in range(per):
            in_own(f, ri).wait()
            for d in range(1, n):
                in_copy(f, ri, d).wait_recv()

        def shift_loop(ri, carry):
            mine = jnp.where(ri == 0, radius(me, 0), radius(me, 1))
            offset = jnp.full((8, LANES), offs_ref[mine], jnp.int32)
            weight = jnp.broadcast_to(coefs[HALO + mine, 4:5, :], (8, LANES))
            keep = 1.0 - weight
            fine = offset & (LANES - 1)

            def shift_rows(group, carry):
                z0 = pl.multiple_of(group * 8, 8)
                cells = [
                    loops[f, t // tiles, ri, pl.ds(z0, 8), (t % tiles) * LANES : (t % tiles + 1) * LANES]
                    for t in range(loop_tiles)
                ]
                step = 1
                while step < LANES:
                    taken = (offset & step) != 0
                    cells = [jnp.where(taken, pltpu.roll(c, step, 1), c) for c in cells]
                    step *= 2
                inside = lane8 < fine
                cells = [
                    jnp.where(inside, cells[t - 1], cells[t]) for t in range(loop_tiles)
                ]
                step = 1
                while step < loop_tiles:
                    taken = (offset & (step * LANES)) != 0
                    cells = [
                        jnp.where(taken, cells[t - step], cells[t]) for t in range(loop_tiles)
                    ]
                    step *= 2
                turned = [pltpu.roll(c, 1, 1) for c in cells]
                moved = [
                    keep * cells[t] + weight * jnp.where(lane8 == 0, turned[t - 1], turned[t])
                    for t in range(loop_tiles)
                ]
                for t in range(loop_tiles):
                    at = (t % tiles) * LANES
                    stage[f, t // tiles, ri, pl.ds(z0, 8), at : at + LANES] = moved[t]
                for q in range(n):
                    right = moved[(tiles * q + tiles) % loop_tiles]
                    both = jnp.where(lane8 < LANES // 2, right, moved[tiles * q - 1])
                    pack[ri, q, pl.ds(z0, 8), :] = both
                return carry

            return lax.fori_loop(0, nz // 8, shift_rows, carry)

        lax.fori_loop(0, per, shift_loop, 0)

        def pack_edges(q, carry):
            tile = pltpu.roll(pack[0, q], 2, 1)
            for ri in range(1, per):
                tile = jnp.where(lane < 4 * ri, tile, pltpu.roll(pack[ri, q], 2 + 4 * ri, 1))
            square = jnp.concatenate([tile] * (LANES // nz), axis=0).T
            edge_stage[f, q] = square[0 : 4 * per]
            return carry

        lax.fori_loop(0, n, pack_edges, 0)
        edge_own(f).start()
        for d in range(1, n):
            edge_copy(f, d).start()
        for ri in range(per):
            back_own(f, ri).start()
            for d in range(1, n):
                back_copy(f, ri, d).start()
        return carry

    lax.fori_loop(0, fields, shift_field, 0)

    @pl.when(has_low)
    def _():
        coef_copy(False).wait_recv()

    @pl.when(has_high)
    def _():
        coef_copy(True).wait_recv()

    def blend(cur, prev_tile, next_tile, up, low, where_r, height, height2):
        k_up = coefs[where_r, 0:1, :]
        k_low = coefs[where_r, 1:2, :]
        k_loop = coefs[where_r, 2:3, :]
        k_mid = coefs[where_r, 3:4, :]
        west = jnp.where(lane == 0, pltpu.roll(prev_tile, 1, 1), pltpu.roll(cur, 1, 1))
        east = jnp.where(
            lane == LANES - 1,
            pltpu.roll(next_tile, LANES - 1, 1),
            pltpu.roll(cur, LANES - 1, 1),
        )
        below = jnp.where(zrow == 0, 0.0, pltpu.roll(cur, 1, 0))
        above = jnp.where(zrow == nz - 1, 0.0, pltpu.roll(cur, nz - 1, 0))
        total = (k_mid - height2) * cur + k_up * up + k_low * low
        return total + k_loop * (east + west) + height * (above + below)

    for f in range(fields):
        edge_own(f).wait()
        back_own(f, 0).wait()
        for d in range(1, n):
            edge_copy(f, d).wait_recv()
            back_copy(f, 0, d).wait_recv()

        @pl.when(has_low)
        def _(f=f):
            for copy in halo_copies(f, True):
                copy.start()

        @pl.when(has_high)
        def _(f=f):
            for copy in halo_copies(f, False):
                copy.start()

        @pl.when(has_low)
        def _(f=f):
            for copy in halo_copies(f, False):
                copy.wait_recv()

        @pl.when(has_high)
        def _(f=f):
            for copy in halo_copies(f, True):
                copy.wait_recv()

        lines = edges[f].reshape((n + 2 * HALO) * 4 * per, LANES)
        square = jnp.concatenate([lines, lines[0 : LANES - lines.shape[0]]], axis=0).T[0:nz]
        for i in range(radii + 2 * HALO):
            r = i - HALO
            if r < half:
                at = 8 * i
            elif r < half + n:
                at = 8 * (HALO + r - half) + 4
            else:
                at = 8 * (HALO + r - radii + n)
            extra[i] = pltpu.roll(square, (2 * LANES - 2 - at) % LANES, 1)

        def first(i, carry, f=f):
            height = height_ref[...]
            height2 = height + height

            def tile(r, t):
                if t == tiles:
                    return extra[r]
                return state[f, r, :, pl.ds(t * LANES, LANES)]

            for t in range(tiles + 1):
                mid[i - 1, :, pl.ds(t * LANES, LANES)] = blend(
                    tile(i, t),
                    tile(i, (t + tiles) % (tiles + 1)),
                    tile(i, (t + 1) % (tiles + 1)),
                    tile(i + 1, t),
                    tile(i - 1, t),
                    i,
                    height,
                    height2,
                )
            return carry

        lax.fori_loop(1, half + 1, first, 0)
        lax.fori_loop(radii + 2 * HALO - 1 - half, radii + 2 * HALO - 1, first, 0)

        @pl.when(jnp.logical_not(has_low))
        def _():
            mid[0] = jnp.zeros(mid.shape[1:], jnp.float32)

        @pl.when(jnp.logical_not(has_high))
        def _():
            mid[radii + 1] = jnp.zeros(mid.shape[1:], jnp.float32)

        def second(i, carry, f=f):
            height = height_ref[...]
            height2 = height + height

            def tile(r, t):
                return mid[r, :, pl.ds(t * LANES, LANES)]

            for t in range(tiles):
                out_ref[f, i - 1, :, pl.ds(t * LANES, LANES)] = blend(
                    tile(i, t),
                    tile(i, (t + tiles) % (tiles + 1)),
                    tile(i, (t + 1) % (tiles + 1)),
                    tile(i + 1, t),
                    tile(i - 1, t),
                    i + 1,
                    height,
                    height2,
                )
            return carry

        lax.fori_loop(1, half - 1, second, 0)
        lax.fori_loop(radii - half + 3, radii + 1, second, 0)
        back_own(f, 1).wait()
        for d in range(1, n):
            back_copy(f, 1, d).wait_recv()
        lax.fori_loop(half + 1, radii + 2 * HALO - 1 - half, first, 0)
        lax.fori_loop(half - 1, radii - half + 3, second, 0)

    for f in range(fields):
        for d in range(1, n):
            edge_copy(f, d).wait_send()
            for ri in range(per):
                in_copy(f, ri, d).wait_send()
                back_copy(f, ri, d).wait_send()

        @pl.when(has_low)
        def _(f=f):
            for copy in halo_copies(f, True):
                copy.wait_send()

        @pl.when(has_high)
        def _(f=f):
            for copy in halo_copies(f, False):
                copy.wait_send()

    @pl.when(has_low)
    def _():
        coef_copy(True).wait_send()

    @pl.when(has_high)
    def _():
        coef_copy(False).wait_send()


def local(n, rows, fields, offsets, fraction, radial_diff, radial_drift, loop_diff, height_diff):
    count, radii, nz, width = fields.shape
    per = radii // n
    full = radii + 2 * HALO
    wide = width + LANES
    f32 = jnp.float32
    dma = pltpu.SemaphoreType.DMA
    scratch = [
        pltpu.VMEM((count, n, per, nz, width), f32),
        pltpu.VMEM((count, n, per, nz, width), f32),
        pltpu.VMEM((per, n, nz, LANES), f32),
        pltpu.VMEM((count, n, 4 * per, LANES), f32),
        pltpu.VMEM((count, full, nz, width), f32),
        pltpu.VMEM((count, n + 2 * HALO, 4 * per, LANES), f32),
        pltpu.VMEM((full, nz, LANES), f32),
        pltpu.VMEM((full - 2, nz, wide), f32),
        pltpu.VMEM((full, 8, LANES), f32),
        pltpu.VMEM((nz, LANES), f32),
        pltpu.SMEM((radii,), jnp.int32),
        pltpu.SMEM((radii,), f32),
        pltpu.SMEM((radii,), f32),
        pltpu.SMEM((radii,), f32),
        pltpu.SMEM((radii,), f32),
        pltpu.SMEM((nz,), f32),
        dma((6,)),
        dma((count, per, n)),
        dma((count, per, n)),
        dma((count, per, n)),
        dma((count, per, n)),
        dma((count, n)),
        dma((count, n)),
        dma((count, 2, 2)),
        dma((count, 2, 2)),
        dma((4,)),
        dma((count, per)),
    ]
    hbm = pl.BlockSpec(memory_space=pltpu.HBM)
    return pl.pallas_call(
        functools.partial(kernel, n, rows),
        out_shape=pltpu.VMEM(fields.shape, f32),
        in_specs=[hbm] * 7,
        out_specs=pl.BlockSpec(memory_space=pltpu.VMEM),
        scratch_shapes=scratch,
        compiler_params=pltpu.CompilerParams(
            collective_id=0, has_side_effects=True, vmem_limit_bytes=56557568
        ),
    )(offsets, fraction, radial_diff, radial_drift, loop_diff, height_diff, fields)


def solution(mesh):
    placed = (P(None, "row", None, "phi"), P("row"), P("row"), P("row"), P("row"), P("row"), P())
    body = functools.partial(local, mesh.shape["phi"], mesh.shape["row"])
    return jax.shard_map(
        body, mesh=mesh, in_specs=placed, out_specs=P(None, "row", None, "phi"), check_vma=False
    )
```

```python
import functools

import jax
import jax.numpy as jnp
from jax import lax
from jax.experimental import pallas as pl
from jax.experimental.pallas import tpu as pltpu
from jax.sharding import PartitionSpec as P

LANES = 128
HALO = 2
MESH = pl.DeviceIdType.MESH


def kernel(
    n,
    rows,
    offs_in,
    frac_in,
    diff_in,
    drift_in,
    loop_in,
    rise_in,
    fields_ref,
    out_ref,
    *scratch,
):
    fields, radii, nz, width = fields_ref.shape
    per = radii // n
    half = n // 2
    tiles = width // LANES
    loop_tiles = tiles * n
    (
        loops,
        stage,
        pack,
        edge_stage,
        state,
        edges,
        extra,
        mid,
        coefs,
        height_ref,
        offs_ref,
        frac_ref,
        diff_ref,
        drift_ref,
        loop_ref,
        rise_ref,
        small_sem,
        in_send,
        in_recv,
        back_send,
        back_recv,
        edge_send,
        edge_recv,
        halo_send,
        halo_recv,
        coef_sem,
        own_sem,
    ) = scratch
    smalls = [
        pltpu.make_async_copy(source, target, small_sem.at[i])
        for i, (source, target) in enumerate(
            (
                (offs_in, offs_ref),
                (frac_in, frac_ref),
                (diff_in, diff_ref),
                (drift_in, drift_ref),
                (loop_in, loop_ref),
                (rise_in, rise_ref),
            )
        )
    ]
    for copy in smalls:
        copy.start()
    me = lax.axis_index("phi")
    row = lax.axis_index("row")
    has_low = row > 0
    has_high = row < rows - 1
    lane = lax.broadcasted_iota(jnp.int32, (nz, LANES), 1)
    zrow = lax.broadcasted_iota(jnp.int32, (nz, LANES), 0)

    barrier = pltpu.get_barrier_semaphore()
    for d in range(1, n):
        pl.semaphore_signal(
            barrier, inc=1, device_id={"phi": lax.rem(me + d, n)}, device_id_type=MESH
        )

    @pl.when(has_low)
    def _():
        pl.semaphore_signal(barrier, inc=1, device_id={"row": row - 1}, device_id_type=MESH)

    @pl.when(has_high)
    def _():
        pl.semaphore_signal(barrier, inc=1, device_id={"row": row + 1}, device_id_type=MESH)

    inner = jnp.logical_and(has_low, has_high)

    @pl.when(inner)
    def _():
        pl.semaphore_wait(barrier, n + 1)

    @pl.when(jnp.logical_not(inner))
    def _():
        pl.semaphore_wait(barrier, n)

    order = sorted(range(2, n), key=lambda d: (d % 2, -d)) + [1]

    def partner(d):
        bits = n.bit_length() - 1
        return sum(
            lax.rem(me // (1 << k) + ((d >> k) & 1), 2) * (1 << k) for k in range(bits)
        )

    def radius(owner, ri):
        if ri == 1:
            return owner + half
        return jnp.where(owner < half, owner, owner + radii - n)

    def in_own(f, ri):
        return pltpu.make_async_copy(
            fields_ref.at[f, radius(me, ri)], loops.at[f, me, ri], own_sem.at[f, ri]
        )

    def in_copy(f, ri, d):
        to = partner(d)
        return pltpu.make_async_remote_copy(
            src_ref=fields_ref.at[f, radius(to, ri)],
            dst_ref=loops.at[f, me, ri],
            send_sem=in_send.at[f, ri, d],
            recv_sem=in_recv.at[f, ri, d],
            device_id={"phi": to},
            device_id_type=MESH,
        )

    def back_copy(f, ri, d):
        to = partner(d)
        return pltpu.make_async_remote_copy(
            src_ref=stage.at[f, to, ri],
            dst_ref=state.at[f, HALO + radius(me, ri)],
            send_sem=back_send.at[f, ri, d],
            recv_sem=back_recv.at[f, ri, d],
            device_id={"phi": to},
            device_id_type=MESH,
        )

    def edge_copy(f, d):
        to = partner(d)
        return pltpu.make_async_remote_copy(
            src_ref=edge_stage.at[f, to],
            dst_ref=edges.at[f, me + HALO],
            send_sem=edge_send.at[f, d],
            recv_sem=edge_recv.at[f, d],
            device_id={"phi": to},
            device_id_type=MESH,
        )

    def back_own(f, ri):
        return pltpu.make_async_copy(
            stage.at[f, me, ri], state.at[f, HALO + radius(me, ri)], back_send.at[f, ri, 0]
        )

    def edge_own(f):
        return pltpu.make_async_copy(
            edge_stage.at[f, me], edges.at[f, me + HALO], edge_send.at[f, 0]
        )

    def halo_copies(f, low):
        side = 0 if low else 1
        source = HALO if low else radii
        target = radii + HALO if low else 0
        to = row - 1 if low else row + 1
        return (
            pltpu.make_async_remote_copy(
                src_ref=state.at[f, pl.ds(source, HALO)],
                dst_ref=state.at[f, pl.ds(target, HALO)],
                send_sem=halo_send.at[f, side, 0],
                recv_sem=halo_recv.at[f, side, 0],
                device_id={"row": to},
                device_id_type=MESH,
            ),
            pltpu.make_async_remote_copy(
                src_ref=edges.at[f, pl.ds(HALO if low else n, HALO)],
                dst_ref=edges.at[f, pl.ds(n + HALO if low else 0, HALO)],
                send_sem=halo_send.at[f, side, 1],
                recv_sem=halo_recv.at[f, side, 1],
                device_id={"row": to},
                device_id_type=MESH,
            ),
        )

    def coef_copy(low):
        side = 0 if low else 1
        return pltpu.make_async_remote_copy(
            src_ref=coefs.at[pl.ds(HALO if low else radii, HALO)],
            dst_ref=coefs.at[pl.ds(radii + HALO if low else 0, HALO)],
            send_sem=coef_sem.at[side],
            recv_sem=coef_sem.at[2 + side],
            device_id={"row": row - 1 if low else row + 1},
            device_id_type=MESH,
        )

    for f in range(fields):
        for ri in range(per):
            for d in order:
                in_copy(f, ri, d).start()
            in_own(f, ri).start()

    for copy in smalls:
        copy.wait()

    def fill_coefs(i, carry):
        diff = jnp.full((1, LANES), diff_ref[i], jnp.float32)
        drift = jnp.full((1, LANES), drift_ref[i], jnp.float32)
        loop = jnp.full((1, LANES), loop_ref[i], jnp.float32)
        coefs[HALO + i, 0:1, :] = diff + drift
        coefs[HALO + i, 1:2, :] = diff - drift
        coefs[HALO + i, 2:3, :] = loop
        coefs[HALO + i, 3:4, :] = 1.0 - 2.0 * (diff + loop)
        coefs[HALO + i, 4:5, :] = jnp.full((1, LANES), frac_ref[i], jnp.float32)
        coefs[HALO + i, 5:8, :] = jnp.zeros((3, LANES), jnp.float32)
        return carry

    lax.fori_loop(0, radii, fill_coefs, 0)

    def fill_height(z, carry):
        height_ref[pl.ds(z, 1), :] = jnp.full((1, LANES), rise_ref[z], jnp.float32)
        return carry

    lax.fori_loop(0, nz, fill_height, 0)

    @pl.when(has_low)
    def _():
        coef_copy(True).start()

    @pl.when(has_high)
    def _():
        coef_copy(False).start()


    @pl.when(jnp.logical_not(has_low))
    def _():
        state[:, 0:HALO] = jnp.zeros((fields, HALO, nz, width), jnp.float32)
        edges[:, 0:HALO] = jnp.zeros((fields, HALO) + edges.shape[2:], jnp.float32)
        coefs[0:HALO] = jnp.zeros((HALO,) + coefs.shape[1:], jnp.float32)

    @pl.when(jnp.logical_not(has_high))
    def _():
        state[:, radii + HALO :] = jnp.zeros((fields, HALO, nz, width), jnp.float32)
        edges[:, n + HALO :] = jnp.zeros((fields, HALO) + edges.shape[2:], jnp.float32)
        coefs[radii + HALO :] = jnp.zeros((HALO,) + coefs.shape[1:], jnp.float32)

    lane8 = lax.broadcasted_iota(jnp.int32, (8, LANES), 1)

    def shift_field(f, carry):
        for ri in range(per):
            in_own(f, ri).wait()
            for d in order:
                in_copy(f, ri, d).wait_recv()

        def shift_loop(ri, carry):
            mine = jnp.where(ri == 0, radius(me, 0), radius(me, 1))
            offset = jnp.full((8, LANES), offs_ref[mine], jnp.int32)
            weight = jnp.broadcast_to(coefs[HALO + mine, 4:5, :], (8, LANES))
            keep = 1.0 - weight
            fine = offset & (LANES - 1)

            def shift_rows(group, carry):
                z0 = pl.multiple_of(group * 8, 8)
                cells = [
                    loops[f, t // tiles, ri, pl.ds(z0, 8), (t % tiles) * LANES : (t % tiles + 1) * LANES]
                    for t in range(loop_tiles)
                ]
                step = 1
                while step < LANES:
                    taken = (offset & step) != 0
                    cells = [jnp.where(taken, pltpu.roll(c, step, 1), c) for c in cells]
                    step *= 2
                inside = lane8 < fine
                cells = [
                    jnp.where(inside, cells[t - 1], cells[t]) for t in range(loop_tiles)
                ]
                step = 1
                while step < loop_tiles:
                    taken = (offset & (step * LANES)) != 0
                    cells = [
                        jnp.where(taken, cells[t - step], cells[t]) for t in range(loop_tiles)
                    ]
                    step *= 2
                turned = [pltpu.roll(c, 1, 1) for c in cells]
                moved = [
                    keep * cells[t] + weight * jnp.where(lane8 == 0, turned[t - 1], turned[t])
                    for t in range(loop_tiles)
                ]
                for t in range(loop_tiles):
                    at = (t % tiles) * LANES
                    stage[f, t // tiles, ri, pl.ds(z0, 8), at : at + LANES] = moved[t]
                for q in range(n):
                    right = moved[(tiles * q + tiles) % loop_tiles]
                    both = jnp.where(lane8 < LANES // 2, right, moved[tiles * q - 1])
                    pack[ri, q, pl.ds(z0, 8), :] = both
                return carry

            return lax.fori_loop(0, nz // 8, shift_rows, carry)

        lax.fori_loop(0, per, shift_loop, 0)

        def pack_edges(q, carry):
            tile = pltpu.roll(pack[0, q], 2, 1)
            for ri in range(1, per):
                tile = jnp.where(lane < 4 * ri, tile, pltpu.roll(pack[ri, q], 2 + 4 * ri, 1))
            square = jnp.concatenate([tile] * (LANES // nz), axis=0).T
            edge_stage[f, q] = square[0 : 4 * per]
            return carry

        lax.fori_loop(0, n, pack_edges, 0)
        edge_own(f).start()
        for d in order:
            edge_copy(f, d).start()
        for ri in range(per):
            back_own(f, ri).start()
            for d in order:
                back_copy(f, ri, d).start()
        return carry

    lax.fori_loop(0, fields, shift_field, 0)

    @pl.when(has_low)
    def _():
        coef_copy(False).wait_recv()

    @pl.when(has_high)
    def _():
        coef_copy(True).wait_recv()

    def blend(cur, prev_tile, next_tile, up, low, where_r, height, height2):
        k_up = coefs[where_r, 0:1, :]
        k_low = coefs[where_r, 1:2, :]
        k_loop = coefs[where_r, 2:3, :]
        k_mid = coefs[where_r, 3:4, :]
        west = jnp.where(lane == 0, pltpu.roll(prev_tile, 1, 1), pltpu.roll(cur, 1, 1))
        east = jnp.where(
            lane == LANES - 1,
            pltpu.roll(next_tile, LANES - 1, 1),
            pltpu.roll(cur, LANES - 1, 1),
        )
        below = jnp.where(zrow == 0, 0.0, pltpu.roll(cur, 1, 0))
        above = jnp.where(zrow == nz - 1, 0.0, pltpu.roll(cur, nz - 1, 0))
        total = (k_mid - height2) * cur + k_up * up + k_low * low
        return total + k_loop * (east + west) + height * (above + below)

    for f in range(fields):
        edge_own(f).wait()
        back_own(f, 0).wait()
        for d in order:
            edge_copy(f, d).wait_recv()
            back_copy(f, 0, d).wait_recv()

        @pl.when(has_low)
        def _(f=f):
            for copy in halo_copies(f, True):
                copy.start()

        @pl.when(has_high)
        def _(f=f):
            for copy in halo_copies(f, False):
                copy.start()

        @pl.when(has_low)
        def _(f=f):
            for copy in halo_copies(f, False):
                copy.wait_recv()

        @pl.when(has_high)
        def _(f=f):
            for copy in halo_copies(f, True):
                copy.wait_recv()

        lines = edges[f].reshape((n + 2 * HALO) * 4 * per, LANES)
        square = jnp.concatenate([lines, lines[0 : LANES - lines.shape[0]]], axis=0).T[0:nz]
        for i in range(radii + 2 * HALO):
            r = i - HALO
            if r < half:
                at = 8 * i
            elif r < half + n:
                at = 8 * (HALO + r - half) + 4
            else:
                at = 8 * (HALO + r - radii + n)
            extra[i] = pltpu.roll(square, (2 * LANES - 2 - at) % LANES, 1)

        def first(i, carry, f=f):
            height = height_ref[...]
            height2 = height + height

            def tile(r, t):
                if t == tiles:
                    return extra[r]
                return state[f, r, :, pl.ds(t * LANES, LANES)]

            for t in range(tiles + 1):
                mid[i - 1, :, pl.ds(t * LANES, LANES)] = blend(
                    tile(i, t),
                    tile(i, (t + tiles) % (tiles + 1)),
                    tile(i, (t + 1) % (tiles + 1)),
                    tile(i + 1, t),
                    tile(i - 1, t),
                    i,
                    height,
                    height2,
                )
            return carry

        lax.fori_loop(1, half + 1, first, 0)
        lax.fori_loop(radii + 2 * HALO - 1 - half, radii + 2 * HALO - 1, first, 0)

        @pl.when(jnp.logical_not(has_low))
        def _():
            mid[0] = jnp.zeros(mid.shape[1:], jnp.float32)

        @pl.when(jnp.logical_not(has_high))
        def _():
            mid[radii + 1] = jnp.zeros(mid.shape[1:], jnp.float32)

        def second(i, carry, f=f):
            height = height_ref[...]
            height2 = height + height

            def tile(r, t):
                return mid[r, :, pl.ds(t * LANES, LANES)]

            for t in range(tiles):
                out_ref[f, i - 1, :, pl.ds(t * LANES, LANES)] = blend(
                    tile(i, t),
                    tile(i, (t + tiles) % (tiles + 1)),
                    tile(i, (t + 1) % (tiles + 1)),
                    tile(i + 1, t),
                    tile(i - 1, t),
                    i + 1,
                    height,
                    height2,
                )
            return carry

        lax.fori_loop(1, half - 1, second, 0)
        lax.fori_loop(radii - half + 3, radii + 1, second, 0)
        back_own(f, 1).wait()
        for d in order:
            back_copy(f, 1, d).wait_recv()
        lax.fori_loop(half + 1, radii + 2 * HALO - 1 - half, first, 0)
        lax.fori_loop(half - 1, radii - half + 3, second, 0)

    for f in range(fields):
        for d in order:
            edge_copy(f, d).wait_send()
            for ri in range(per):
                in_copy(f, ri, d).wait_send()
                back_copy(f, ri, d).wait_send()

        @pl.when(has_low)
        def _(f=f):
            for copy in halo_copies(f, True):
                copy.wait_send()

        @pl.when(has_high)
        def _(f=f):
            for copy in halo_copies(f, False):
                copy.wait_send()

    @pl.when(has_low)
    def _():
        coef_copy(True).wait_send()

    @pl.when(has_high)
    def _():
        coef_copy(False).wait_send()


def local(n, rows, fields, offsets, fraction, radial_diff, radial_drift, loop_diff, height_diff):
    count, radii, nz, width = fields.shape
    per = radii // n
    full = radii + 2 * HALO
    wide = width + LANES
    f32 = jnp.float32
    dma = pltpu.SemaphoreType.DMA
    scratch = [
        pltpu.VMEM((count, n, per, nz, width), f32),
        pltpu.VMEM((count, n, per, nz, width), f32),
        pltpu.VMEM((per, n, nz, LANES), f32),
        pltpu.VMEM((count, n, 4 * per, LANES), f32),
        pltpu.VMEM((count, full, nz, width), f32),
        pltpu.VMEM((count, n + 2 * HALO, 4 * per, LANES), f32),
        pltpu.VMEM((full, nz, LANES), f32),
        pltpu.VMEM((full - 2, nz, wide), f32),
        pltpu.VMEM((full, 8, LANES), f32),
        pltpu.VMEM((nz, LANES), f32),
        pltpu.SMEM((radii,), jnp.int32),
        pltpu.SMEM((radii,), f32),
        pltpu.SMEM((radii,), f32),
        pltpu.SMEM((radii,), f32),
        pltpu.SMEM((radii,), f32),
        pltpu.SMEM((nz,), f32),
        dma((6,)),
        dma((count, per, n)),
        dma((count, per, n)),
        dma((count, per, n)),
        dma((count, per, n)),
        dma((count, n)),
        dma((count, n)),
        dma((count, 2, 2)),
        dma((count, 2, 2)),
        dma((4,)),
        dma((count, per)),
    ]
    hbm = pl.BlockSpec(memory_space=pltpu.HBM)
    return pl.pallas_call(
        functools.partial(kernel, n, rows),
        out_shape=pltpu.VMEM(fields.shape, f32),
        in_specs=[hbm] * 7,
        out_specs=pl.BlockSpec(memory_space=pltpu.VMEM),
        scratch_shapes=scratch,
        compiler_params=pltpu.CompilerParams(
            collective_id=0, has_side_effects=True, vmem_limit_bytes=56557568
        ),
    )(offsets, fraction, radial_diff, radial_drift, loop_diff, height_diff, fields)


def solution(mesh):
    placed = (P(None, "row", None, "phi"), P("row"), P("row"), P("row"), P("row"), P("row"), P())
    body = functools.partial(local, mesh.shape["phi"], mesh.shape["row"])
    return jax.shard_map(
        body, mesh=mesh, in_specs=placed, out_specs=P(None, "row", None, "phi"), check_vma=False
    )
```
